32 devices in a mesh: sample: 4 (over z), spatial: 4 (over x, core), channel: 2 (over y).
Axes of the slice: x: 2, y: 2, z: 4, core: 2. Of those that a mesh axis runs over, the one named last changes fastest.
Arguments:
- volume: bfloat16 [4, 32, 32, 256], P('sample', 'channel', 'spatial'), may hold values from -6 to 6
- kernel_mid: bfloat16 [27, 64, 128], replicated, may hold values from -0.15625 to 0.15625
- kernel_top: bfloat16 [27, 256, 128], P(None, 'channel'), may hold values from -0.3125 to 0.3125
- upstream: bfloat16 [4, 8, 8, 1, 256], P('sample', None, 'spatial', None, 'channel'), may hold values from -1.5 to 1.5
Outputs:
- block_out: bfloat16 [4, 8, 8, 1, 256], P('sample', None, 'spatial', None, 'channel')
- grad_mid: float32 [1728, 128], P('channel')
- grad_top: float32 [27, 256, 128], P(None, 'channel')
The draws below stay inside these ranges and needn't reach their ends.
All inputs are finite; a program needn't handle non-finite values.
Results may differ from the reference program's by a relative error of at most 0.0054.
Values may be sent and summed in bfloat16 or wider, within the bound.
A program may use at most 64 MiB of HBM per device.

```python
import jax
import jax.numpy as jnp
from jax import lax

C_IN = 64
C_MID = 128
C_OUT = 256
WID = 4
BATCH = 4
HEIGHT = 32
DEPTH = 32


def steps_of(rng, shape, split, smallest, high):
    gain = 1.0
    for position, shards_of in split:
        heights = jax.random.uniform(jax.random.fold_in(jax.random.fold_in(rng, 6), position), (shards_of,), jnp.float32, smallest / len(split), high / len(split))
        gain = gain * jnp.repeat(jnp.exp(heights), shape[position] // shards_of).reshape((-1,) + (1,) * (len(shape) - 1 - position))
    return gain


def bell_draw(rng, extent, deviation, most, split=(), kind=jnp.bfloat16):
    entries = jax.random.normal(rng, extent, jnp.float32) * deviation
    if len(split) > 0:
        entries = steps_of(rng, extent, split, -0.22, 0.18) * entries
    return jnp.clip(entries, min=-most, max=most).astype(kind)


def setup_inputs(seed: int = 0) -> dict:
    seeds = jax.random.split(jax.random.key(seed), 5)
    return {
        "volume": bell_draw(seeds[0], (BATCH, HEIGHT, DEPTH, WID * C_IN), 1.0, 6.0, ((0, 4), (1, 2), (2, 4))),
        "kernel_mid": bell_draw(seeds[1], (27, C_IN, C_MID), (27 * C_IN) ** -0.5, 0.15625),
        "kernel_top": bell_draw(seeds[2], (27, C_OUT, C_MID), (27 * C_MID // 8) ** -0.5, 0.3125, ((1, 2),)),
        "upstream": bell_draw(seeds[3], (BATCH, HEIGHT // 4, DEPTH // 4, WID // 4, C_OUT), 0.25, 1.5, ((0, 4), (2, 4), (4, 2))),
    }


def slope(values):
    sig = jax.nn.sigmoid(values)
    return sig * (1.0 + values * (1.0 - sig))

def pool_mean(field):
    h_size, d_size, w_size, c_size = field.shape
    blocks = field.reshape(h_size // 2, 2, d_size // 2, 2, w_size // 2, 2, c_size)
    return lax.optimization_barrier(jnp.mean(blocks, axis=(1, 3, 5)))

def spread(field):
    h_size, d_size, w_size, c_size = field.shape
    wide = jnp.broadcast_to(field[:, None, :, None, :, None, :], (h_size, 2, d_size, 2, w_size, 2, c_size))
    return wide.reshape(2 * h_size, 2 * d_size, 2 * w_size, c_size) * 0.125

def pad_all(field):
    return jnp.pad(field, ((1, 1), (1, 1), (1, 1), (0, 0)))

def convolve(padded, kernel, row_count, depth_count, width_count):
    running = jnp.zeros((row_count * depth_count * width_count, kernel.shape[2]), jnp.float32)
    for off_depth in range(3):
        for off_rows in range(3):
            for off_width in range(3):
                sliced = padded[off_rows:off_rows + row_count, off_depth:off_depth + depth_count, off_width:off_width + width_count, :]
                sliced = sliced.reshape(row_count * depth_count * width_count, padded.shape[3])
                running = running + jnp.dot(sliced, kernel[9 * off_depth + 3 * off_rows + off_width], preferred_element_type=jnp.float32)
    return running.reshape(row_count, depth_count, width_count, kernel.shape[2])

def kernel_grad(padded, grads, row_count, depth_count, width_count):
    flat = grads.reshape(row_count * depth_count * width_count, grads.shape[3])
    pieces = []
    for off_depth in range(3):
        for off_rows in range(3):
            for off_width in range(3):
                sliced = padded[off_rows:off_rows + row_count, off_depth:off_depth + depth_count, off_width:off_width + width_count, :]
                sliced = sliced.reshape(row_count * depth_count * width_count, padded.shape[3])
                pieces.append(lax.dot_general(sliced, flat, (((0,), (0,)), ((), ())), preferred_element_type=jnp.float32))
    return jnp.stack(pieces)

def back_convolve(padded, kernel, row_count, depth_count, width_count):
    running = jnp.zeros((row_count * depth_count * width_count, kernel.shape[1]), jnp.float32)
    for off_depth in range(3):
        for off_rows in range(3):
            for off_width in range(3):
                sliced = padded[2 - off_rows:2 - off_rows + row_count, 2 - off_depth:2 - off_depth + depth_count, 2 - off_width:2 - off_width + width_count, :]
                sliced = sliced.reshape(row_count * depth_count * width_count, padded.shape[3])
                running = running + lax.dot_general(sliced, kernel[9 * off_depth + 3 * off_rows + off_width], (((1,), (1,)), ((), ())), preferred_element_type=jnp.float32)
    return running.reshape(row_count, depth_count, width_count, kernel.shape[1])

def reference(volume, kernel_mid, kernel_top, upstream):
    channel_in = kernel_mid.shape[1]
    height_all = volume.shape[1]
    depth_all = volume.shape[2]
    width_all = volume.shape[3] // channel_in
    turned = jnp.transpose(kernel_top, (0, 2, 1))

    def one_sample(carry, inputs):
        sample_volume, sample_upper = inputs
        cells = sample_volume.reshape(height_all, depth_all, width_all, channel_in)
        padded = pad_all(cells)
        pre_mid = convolve(padded, kernel_mid, height_all, depth_all, width_all)
        pooled = pool_mean(jax.nn.silu(pre_mid)).astype(jnp.bfloat16)
        top_pad = pad_all(pooled)
        pre_top = convolve(top_pad, turned, height_all // 2, depth_all // 2, width_all // 2)
        block_out = pool_mean(jax.nn.silu(pre_top)).astype(jnp.bfloat16)
        grad_pre_top = (spread(sample_upper.astype(jnp.float32)) * slope(pre_top)).astype(jnp.bfloat16)
        top_part = kernel_grad(top_pad, grad_pre_top, height_all // 2, depth_all // 2, width_all // 2)
        grad_pooled = back_convolve(pad_all(grad_pre_top), turned, height_all // 2, depth_all // 2, width_all // 2)
        grad_pre_mid = (spread(grad_pooled) * slope(pre_mid)).astype(jnp.bfloat16)
        mid_part = kernel_grad(padded, grad_pre_mid, height_all, depth_all, width_all)
        return ((carry[0] + mid_part, carry[1] + top_part), block_out)
    start_mid = jnp.zeros((27, kernel_mid.shape[1], kernel_mid.shape[2]), jnp.float32)
    start_top = jnp.zeros((27, turned.shape[1], turned.shape[2]), jnp.float32)
    totals, outputs = lax.scan(one_sample, (start_mid, start_top), (volume, upstream))
    grad_mid = totals[0].reshape(27 * kernel_mid.shape[1], kernel_mid.shape[2])
    return (outputs, grad_mid, jnp.transpose(totals[1], (0, 2, 1)))
```

```python
import functools

import jax
import jax.numpy as jnp
from jax import lax
from jax.experimental import pallas as pl
from jax.experimental.pallas import tpu as pltpu
from jax.sharding import PartitionSpec as P


def extended(cells, sides, width):
    for axis, dim in sides:
        count = lax.axis_size(axis)
        ends = count - 1
        head = lax.slice_in_dim(cells, 0, width, axis=dim)
        tail = lax.slice_in_dim(cells, cells.shape[dim] - width, cells.shape[dim], axis=dim)
        cells = jnp.concatenate(
            [
                lax.ppermute(tail, axis, [(i, (i + 1) % count) for i in range(ends)]),
                cells,
                lax.ppermute(head, axis, [((i + 1) % count, i) for i in range(ends)]),
            ],
            axis=dim,
        )
    return cells


def slope(values):
    sig = jax.nn.sigmoid(values)
    return sig * (1.0 + values * (1.0 - sig))


def pool_mean(field):
    h_size, d_size, w_size, c_size = field.shape
    blocks = field.reshape(h_size // 2, 2, d_size // 2, 2, w_size // 2, 2, c_size)
    return jnp.mean(blocks, axis=(1, 3, 5))


def spread(field):
    h_size, d_size, w_size, c_size = field.shape
    wide = jnp.broadcast_to(
        field[:, None, :, None, :, None, :], (h_size, 2, d_size, 2, w_size, 2, c_size)
    )
    return wide.reshape(2 * h_size, 2 * d_size, 2 * w_size, c_size) * 0.125


def width_taps(padded, off_rows, off_depth, row_count, depth_count, width_count, order):
    parts = []
    for off_width in order:
        parts.append(
            padded[
                off_rows : off_rows + row_count,
                off_depth : off_depth + depth_count,
                off_width : off_width + width_count,
                :,
            ]
        )
    joined = jnp.concatenate(parts, axis=3)
    return joined.reshape(row_count * depth_count * width_count, joined.shape[3])


def convolve(padded, kernel, row_count, depth_count, width_count):
    running = jnp.zeros((row_count * depth_count * width_count, kernel.shape[2]), jnp.float32)
    for off_depth in range(3):
        for off_rows in range(3):
            base = 9 * off_depth + 3 * off_rows
            joined = width_taps(
                padded, off_rows, off_depth, row_count, depth_count, width_count, (0, 1, 2)
            )
            stacked = kernel[base : base + 3].reshape(3 * kernel.shape[1], kernel.shape[2])
            running = running + jnp.dot(joined, stacked, preferred_element_type=jnp.float32)
    return running.reshape(row_count, depth_count, width_count, kernel.shape[2])


def convolve_turned(padded, kernel, row_count, depth_count, width_count):
    filters_here = kernel.shape[1]
    running = jnp.zeros((row_count * depth_count * width_count, filters_here), jnp.float32)
    for off_depth in range(3):
        for off_rows in range(3):
            base = 9 * off_depth + 3 * off_rows
            joined = width_taps(
                padded, off_rows, off_depth, row_count, depth_count, width_count, (0, 1, 2)
            )
            stacked = jnp.transpose(kernel[base : base + 3], (0, 2, 1)).reshape(
                3 * kernel.shape[2], filters_here
            )
            running = running + jnp.dot(joined, stacked, preferred_element_type=jnp.float32)
    return running.reshape(row_count, depth_count, width_count, filters_here)


def kernel_grad(padded, grads, row_count, depth_count, width_count):
    flat = grads.reshape(row_count * depth_count * width_count, grads.shape[3])
    pieces = []
    for off_depth in range(3):
        for off_rows in range(3):
            joined = width_taps(
                padded, off_rows, off_depth, row_count, depth_count, width_count, (0, 1, 2)
            )
            pieces.append(
                lax.dot_general(
                    joined, flat, (((0,), (0,)), ((), ())), preferred_element_type=jnp.float32
                )
            )
    stacked = jnp.stack(pieces)
    return stacked.reshape(27, padded.shape[3], grads.shape[3])


def kernel_grad_flipped(padded, grads, row_count, depth_count, width_count):
    flat = grads.reshape(row_count * depth_count * width_count, grads.shape[3])
    channels = padded.shape[3]
    filters_here = grads.shape[3]
    pieces = []
    for off_depth in range(3):
        for off_rows in range(3):
            joined = width_taps(
                padded, off_rows, off_depth, row_count, depth_count, width_count, (0, 1, 2)
            )
            pieces.append(
                lax.dot_general(
                    flat, joined, (((0,), (0,)), ((), ())), preferred_element_type=jnp.float32
                )
            )
    stacked = jnp.stack(pieces).reshape(9, filters_here, 3, channels)
    return jnp.transpose(stacked, (0, 2, 1, 3)).reshape(27, filters_here, channels)


def depth_rim(field):
    return extended(field, (("spatial", 1),), 1)


def pad_sides(field):
    return jnp.pad(field, ((1, 1), (0, 0), (1, 1), (0, 0)))


def share_rows(partial_grad):
    return lax.psum_scatter(partial_grad, "channel", scatter_dimension=0, tiled=True)


def on_device(volume, kernel_mid, kernel_top, upstream):
    channel_in = kernel_mid.shape[1]
    channel_mid = kernel_mid.shape[2]
    row_count = volume.shape[1]
    depth_count = volume.shape[2]
    width_count = volume.shape[3] // channel_in
    cells = volume[0].reshape(row_count, depth_count, width_count, channel_in)
    rimmed = extended(cells, (("spatial", 1), ("channel", 0)), 1)
    padded = jnp.pad(rimmed, ((0, 0), (0, 0), (1, 1), (0, 0)))
    pre_mid = convolve(padded, kernel_mid, row_count, depth_count, width_count)
    pooled = pool_mean(jax.nn.silu(pre_mid)).astype(jnp.bfloat16)
    gathered = lax.all_gather(pooled, "channel", axis=0, tiled=True)
    tall_rows = gathered.shape[0]
    half_depth = depth_count // 2
    half_width = width_count // 2
    top_pad = pad_sides(depth_rim(gathered))
    pre_top = convolve_turned(top_pad, kernel_top, tall_rows, half_depth, half_width)
    block_out = pool_mean(jax.nn.silu(pre_top)).astype(jnp.bfloat16)[None]
    grad_pre_top = (spread(upstream[0].astype(jnp.float32)) * slope(pre_top)).astype(jnp.bfloat16)
    top_part = kernel_grad_flipped(top_pad, grad_pre_top, tall_rows, half_depth, half_width)
    grad_pad = pad_sides(depth_rim(grad_pre_top))
    filters_here = kernel_top.shape[1]
    channel_top = kernel_top.shape[2]
    running = jnp.zeros(
        (lax.axis_size("channel") * (row_count // 2) * half_depth * half_width, channel_top),
        jnp.float32,
    )
    for off_depth in range(3):
        for off_rows in range(3):
            base = 9 * off_depth + 3 * off_rows
            joined = width_taps(
                grad_pad,
                2 - off_rows,
                2 - off_depth,
                lax.axis_size("channel") * (row_count // 2),
                half_depth,
                half_width,
                (2, 1, 0),
            )
            flipped = kernel_top[base : base + 3].reshape(3 * filters_here, channel_top)
            running = running + jnp.dot(joined, flipped, preferred_element_type=jnp.float32)
    grad_pooled = lax.psum_scatter(
        running.reshape(
            lax.axis_size("channel") * (row_count // 2), half_depth, half_width, channel_top
        ),
        "channel",
        scatter_dimension=0,
        tiled=True,
    )
    grad_pre_mid = (spread(grad_pooled) * slope(pre_mid)).astype(jnp.bfloat16)
    mid_part = kernel_grad(padded, grad_pre_mid, row_count, depth_count, width_count).reshape(
        27 * channel_in, channel_mid
    )
    whole_mid, grad_top = lax.psum((mid_part, top_part), ("sample", "spatial"))
    grad_mid = share_rows(whole_mid)
    return (block_out, grad_mid, grad_top)


BF = jnp.bfloat16
F32 = jnp.float32


def fused_body(
    sizes, vol, kmid, ktop, upper, block_out, grad_mid, grad_top,
    vpad, ppad, gpad, xmid, xtop, wmid, wtop, pre, fold0, fold1, part, part_in,
    acc_t, send_a, recv_a, send_b, recv_b, keep_t, send_c, recv_c, all_t,
    acc_m, msend_a, mrecv_a, msend_b, mrecv_b, msend_c, mrecv_c, z_m, all_m,
    ssem, rsem,
):
    samples, slabs, chans = sizes
    b = lax.axis_index("sample")
    s = lax.axis_index("spatial")
    c = lax.axis_index("channel")
    core = lax.rem(s, 2)
    side = lax.div(s, 2)
    s_core = s + 1 - 2 * core
    s_side = s + 2 - 4 * side
    count = [0]

    def place(bb, ss, cc):
        return {"sample": bb, "spatial": ss, "channel": cc}

    def link(source, target, device):
        k = count[0]
        count[0] += 1
        return pltpu.make_async_remote_copy(
            src_ref=source, dst_ref=target, send_sem=ssem.at[k], recv_sem=rsem.at[k],
            device_id=device, device_id_type=pl.DeviceIdType.MESH,
        )

    vpad[...] = jnp.zeros_like(vpad)
    vpad[1:9, 8:24, :] = vol[...]
    ppad[...] = jnp.zeros_like(ppad)
    gpad[...] = jnp.zeros_like(gpad)

    barrier = pltpu.get_barrier_semaphore()
    greeted = 0
    for ds in range(slabs):
        for dc in range(chans):
            if ds or dc:
                pl.semaphore_signal(
                    barrier, inc=1,
                    device_id=place(b, lax.rem(s + ds, slabs), lax.rem(c + dc, chans)),
                    device_id_type=pl.DeviceIdType.MESH,
                )
                greeted += 1
    for db in range(1, samples):
        pl.semaphore_signal(
            barrier, inc=1, device_id=place(lax.rem(b + db, samples), s, c),
            device_id_type=pl.DeviceIdType.MESH,
        )
        greeted += 1
    pl.semaphore_wait(barrier, greeted)

    def inside(value, limit):
        return jnp.logical_and(value >= 0, value < limit)

    planes = {1: (slice(8, 9), slice(0, 1)), 0: (slice(1, 9), slice(1, 9)), -1: (slice(1, 2), slice(9, 10))}
    bands = {1: (slice(16, 24), slice(0, 8)), 0: (slice(8, 24), slice(8, 24)), -1: (slice(8, 16), slice(24, 32))}
    halo = []
    for ds in (0, 1, -1):
        for dc in (0, 1, -1):
            if ds == 0 and dc == 0:
                continue
            copy = link(
                vpad.at[planes[ds][0], bands[dc][0]], vpad.at[planes[ds][1], bands[dc][1]],
                place(b, lax.rem(s + ds + slabs, slabs), lax.rem(c + dc + chans, chans)),
            )
            out_ok = jnp.logical_and(inside(s + ds, slabs), inside(c + dc, chans))
            in_ok = jnp.logical_and(inside(s - ds, slabs), inside(c - dc, chans))
            halo.append((copy, out_ok, in_ok))
    for copy, out_ok, _ in halo:
        @pl.when(out_ok)
        def _(copy=copy):
            copy.start()

    wmid[...] = jnp.zeros_like(wmid)
    for i in range(3):
        for j in range(3):
            for xi in range(4):
                for xo in range(4):
                    l = xi - xo + 1
                    if 0 <= l <= 2:
                        wmid[i, j * 256 + xi * 64 : j * 256 + xi * 64 + 64, xo * 128 : xo * 128 + 128] = kmid[9 * i + 3 * j + l]
            for xi in range(2):
                for xo in range(2):
                    wtop[i, xo * 128 : xo * 128 + 128, j * 256 + xi * 128 : j * 256 + xi * 128 + 128] = ktop[9 * i + 3 * j + xi - xo + 1]
    acc_t[27] = jnp.zeros((4, 32, 128), F32)
    acc_m[0, 27] = jnp.zeros((32, 128), F32)
    acc_m[1, 27] = jnp.zeros((32, 128), F32)

    for copy, out_ok, in_ok in halo:
        @pl.when(out_ok)
        def _(copy=copy):
            copy.wait_send()

        @pl.when(in_ok)
        def _(copy=copy):
            copy.wait_recv()

    for j in range(3):
        xmid[:, :, j * 256 : j * 256 + 256] = vpad[:, 7 + j : 23 + j, :].astype(BF)
    total = jnp.zeros((128, 512), F32)
    for i in range(3):
        total = total + jnp.dot(xmid[i : i + 8].reshape(128, 768), wmid[i], preferred_element_type=F32)
    pre[...] = total
    act = (total / (1.0 + jnp.exp(-total))).reshape(4, 2, 16, 512)
    act = act[:, 0] + act[:, 1]
    fold0[...] = (act[:, :, 0:128] + act[:, :, 128:256]).reshape(64, 128)
    fold1[...] = (act[:, :, 256:384] + act[:, :, 384:512]).reshape(64, 128)
    mine = pl.ds(pl.multiple_of(8 + 8 * c, 8), 8)
    for x, fold in enumerate((fold0, fold1)):
        pooled = (fold[pl.ds(0, 32, 2), :] + fold[pl.ds(1, 32, 2), :]) * 0.125
        ppad[1:5, mine, x * 128 : x * 128 + 128] = pooled.astype(BF).astype(F32).reshape(4, 8, 128)

    swaps = []
    for ds, take, put in ((0, slice(1, 5), slice(1, 5)), (1, slice(4, 5), slice(0, 1)), (-1, slice(1, 2), slice(5, 6))):
        for dc in range(chans):
            if ds == 0 and dc == 0:
                continue
            device = place(b, lax.rem(s + ds + slabs, slabs), lax.rem(c + dc, chans))
            theirs = pl.ds(pl.multiple_of(8 + 8 * lax.rem(c - dc + chans, chans), 8), 8)
            copy = link(ppad.at[take, mine], ppad.at[put, mine], device)
            count[0] -= 1
            back = link(ppad.at[take, theirs], ppad.at[put, theirs], device)
            swaps.append((copy, back, inside(s + ds, slabs), inside(s - ds, slabs)))
    for copy, _, out_ok, _ in swaps:
        @pl.when(out_ok)
        def _(copy=copy):
            copy.start()
    for copy, back, out_ok, in_ok in swaps:
        @pl.when(out_ok)
        def _(copy=copy):
            copy.wait_send()

        @pl.when(in_ok)
        def _(back=back):
            back.wait_recv()

    for j in range(3):
        xtop[:, :, j * 256 : j * 256 + 256] = ppad[:, 7 + j : 23 + j, :].astype(BF)
    top = jnp.zeros((64, 256), F32)
    for i in range(3):
        top = top + lax.dot_general(
            xtop[i : i + 4].reshape(64, 768), wtop[i], (((1,), (1,)), ((), ())), preferred_element_type=F32
        )
    sig = 1.0 / (1.0 + jnp.exp(-top))
    fold1[pl.ds(0, 16, 2), :] = upper[...]
    fold1[pl.ds(1, 16, 2), :] = upper[...]
    wide = fold1[0:32, :].reshape(2, 1, 16, 128)
    wide = jnp.broadcast_to(wide, (2, 2, 16, 128)).reshape(64, 128)
    wide = jnp.concatenate([wide, wide], axis=1) * 0.125
    grads = wide * (sig * (1.0 + top * (1.0 - sig)))
    grads_bf = grads.astype(BF)
    gpad[1:5, 8:24, :] = grads_bf.astype(F32).reshape(4, 16, 256)
    rims = []
    for ds, take, put in ((1, slice(4, 5), slice(0, 1)), (-1, slice(1, 2), slice(5, 6))):
        copy = link(gpad.at[take, 8:24], gpad.at[put, 8:24], place(b, lax.rem(s + ds + slabs, slabs), c))
        rims.append((copy, inside(s + ds, slabs), inside(s - ds, slabs)))
    for copy, out_ok, _ in rims:
        @pl.when(out_ok)
        def _(copy=copy):
            copy.start()
    act = (top / (1.0 + jnp.exp(-top))).reshape(2, 2, 16, 256)
    act = act[:, 0] + act[:, 1]
    fold0[0:32, :] = (act[:, :, 0:128] + act[:, :, 128:256]).reshape(32, 128)
    block_out[...] = (fold0[pl.ds(0, 16, 2), :] + fold0[pl.ds(1, 16, 2), :]) * 0.125

    for i in range(3):
        for j in range(3):
            cross = lax.dot_general(
                grads_bf, xtop[i : i + 4, :, j * 256 : j * 256 + 256].reshape(64, 256),
                (((0,), (0,)), ((), ())), preferred_element_type=F32,
            )
            tap = 9 * i + 3 * j
            acc_t[tap] = cross[128:256, 0:128].reshape(4, 32, 128)
            acc_t[tap + 1] = (cross[0:128, 0:128] + cross[128:256, 128:256]).reshape(4, 32, 128)
            acc_t[tap + 2] = cross[0:128, 128:256].reshape(4, 32, 128)
    send_a[...] = acc_t[:, pl.ds(2 * (1 - core), 2)].astype(BF)
    step_a = link(send_a, recv_a, place(b, s_core, c))
    step_a.start()

    for copy, out_ok, in_ok in rims:
        @pl.when(out_ok)
        def _(copy=copy):
            copy.wait_send()

        @pl.when(in_ok)
        def _(copy=copy):
            copy.wait_recv()
    back_sum = jnp.zeros((64, 256), F32)
    for j in range(3):
        lined = gpad[:, 9 - j : 25 - j, :].astype(BF)
        for i in range(3):
            back_sum = back_sum + jnp.dot(
                lined[2 - i : 6 - i].reshape(64, 256), wtop[i, :, j * 256 : j * 256 + 256], preferred_element_type=F32
            )
    part[...] = back_sum.reshape(4, 16, 256)
    other = 1 - c
    give = link(part.at[:, pl.ds(pl.multiple_of(8 * other, 8), 8)], part_in, place(b, s, other))
    give.start()

    step_a.wait()
    keep_t[...] = acc_t[:, pl.ds(2 * core, 2)] + recv_a[...].astype(F32)
    send_b[...] = keep_t[:, 1 - side].astype(BF)
    step_b = link(send_b, recv_b, place(b, s_side, c))
    step_b.start()

    give.wait()
    pooled_grad = part[:, pl.ds(pl.multiple_of(8 * c, 8), 8)] + part_in[...]
    wides = []
    for x, fold in enumerate((fold0, fold1)):
        half = pooled_grad[:, :, x * 128 : x * 128 + 128].reshape(32, 128)
        fold[pl.ds(0, 32, 2), :] = half
        fold[pl.ds(1, 32, 2), :] = half
        half = jnp.broadcast_to(fold[...].reshape(4, 1, 16, 128), (4, 2, 16, 128)).reshape(128, 128)
        wides += [half, half]
    field = pre[...]
    sig = 1.0 / (1.0 + jnp.exp(-field))
    grads_mid = (jnp.concatenate(wides, axis=1) * 0.125 * (sig * (1.0 + field * (1.0 - sig)))).astype(BF)

    def mid_taps(i):
        for j in range(3):
            cross = lax.dot_general(
                xmid[i : i + 8, :, j * 256 : j * 256 + 256].reshape(128, 256), grads_mid,
                (((0,), (0,)), ((), ())), preferred_element_type=F32,
            )
            for l in range(3):
                block = None
                for xo in range(4):
                    xi = xo + l - 1
                    if 0 <= xi < 4:
                        term = cross[xi * 64 : xi * 64 + 64, xo * 128 : xo * 128 + 128]
                        block = term if block is None else block + term
                for n in range(2):
                    unit = 2 * (9 * i + 3 * j + l) + n
                    acc_m[unit // 27, unit % 27] = block[32 * n : 32 * n + 32]

    mid_taps(0)
    step_b.wait()
    own_t = keep_t[:, side] + recv_b[...].astype(F32)
    keep_t[:, side] = own_t
    send_c[...] = own_t.astype(BF)
    steps_c = []
    for db in range(1, samples):
        to = lax.rem(b + db, samples)
        steps_c.append(link(send_c.at[pl.ds(7 * to, 7)], recv_c.at[db - 1], place(to, s, c)))
    for copy in steps_c:
        copy.start()
    mid_taps(1)
    mid_taps(2)
    msend_a[...] = acc_m[:, pl.ds(14 * (1 - core), 14)].astype(BF)
    mstep_a = link(msend_a, mrecv_a, place(b, s_core, c))
    mstep_a.start()
    for copy in steps_c:
        copy.wait()
    quarter = 2 * core + side
    found = keep_t[pl.ds(7 * b, 7), side]
    for db in range(1, samples):
        found = found + recv_c[db - 1].astype(F32)
    all_t[quarter, pl.ds(7 * b, 7)] = found.astype(BF)
    steps_d = []
    for db in range(1, samples):
        to = lax.rem(b + db, samples)
        frm = lax.rem(b - db + samples, samples)
        spot = all_t.at[quarter, pl.ds(7 * b, 7)]
        copy = link(spot, spot, place(to, s, c))
        count[0] -= 1
        spot = all_t.at[quarter, pl.ds(7 * frm, 7)]
        steps_d.append((copy, link(spot, spot, place(to, s, c))))

    mstep_a.wait()
    kept = acc_m[:, pl.ds(14 * core, 14)] + mrecv_a[...].astype(F32)
    acc_m[:, pl.ds(14 * core, 14)] = kept
    msend_b[...] = acc_m[other, pl.ds(14 * core, 14)].astype(BF)
    mstep_b = link(msend_b, mrecv_b, place(b, s, other))
    mstep_b.start()
    for copy, _ in steps_d:
        copy.start()
    mstep_b.wait()
    near = 14 * core + 7 * side
    far = 14 * core + 7 * (1 - side)
    msend_c[...] = (acc_m[c, pl.ds(far, 7)] + mrecv_b[pl.ds(7 * (1 - side), 7)].astype(F32)).astype(BF)
    mstep_c = link(msend_c, mrecv_c, place(b, s_side, c))
    mstep_c.start()
    mine_m = acc_m[c, pl.ds(near, 7)] + mrecv_b[pl.ds(7 * side, 7)].astype(F32)
    mstep_c.wait()
    z_m[b] = (mine_m + mrecv_c[...].astype(F32)).astype(BF)
    msteps_d = []
    for db in range(1, samples):
        to = lax.rem(b + db, samples)
        frm = lax.rem(b - db + samples, samples)
        copy = link(z_m.at[b], z_m.at[b], place(to, s, c))
        count[0] -= 1
        msteps_d.append((copy, link(z_m.at[frm], z_m.at[frm], place(to, s, c))))
    for copy, _ in msteps_d:
        copy.start()

    for copy, back in steps_d:
        copy.wait_send()
        back.wait_recv()
    mirror = 2 * core + 1 - side
    step_e = link(all_t.at[quarter], all_t.at[quarter], place(b, s_side, c))
    count[0] -= 1
    back_e = link(all_t.at[mirror], all_t.at[mirror], place(b, s_side, c))
    step_e.start()

    for copy, back in msteps_d:
        copy.wait_send()
        back.wait_recv()
    found = z_m[0].astype(F32)
    for k in range(1, samples):
        found = found + z_m[k].astype(F32)
    all_m[pl.ds(near, 7)] = found.astype(BF)
    mstep_e = link(all_m.at[pl.ds(near, 7)], all_m.at[pl.ds(near, 7)], place(b, s_side, c))
    count[0] -= 1
    mback_e = link(all_m.at[pl.ds(far, 7)], all_m.at[pl.ds(far, 7)], place(b, s_side, c))
    mstep_e.start()

    step_e.wait_send()
    back_e.wait_recv()
    near2 = pl.ds(2 * core, 2)
    far2 = pl.ds(2 * (1 - core), 2)
    step_f = link(all_t.at[near2], all_t.at[near2], place(b, s_core, c))
    count[0] -= 1
    back_f = link(all_t.at[far2], all_t.at[far2], place(b, s_core, c))
    step_f.start()

    mstep_e.wait_send()
    mback_e.wait_recv()
    half_near = pl.ds(14 * core, 14)
    half_far = pl.ds(14 * (1 - core), 14)
    mstep_f = link(all_m.at[half_near], all_m.at[half_near], place(b, s_core, c))
    count[0] -= 1
    mback_f = link(all_m.at[half_far], all_m.at[half_far], place(b, s_core, c))
    mstep_f.start()

    step_f.wait_send()
    back_f.wait_recv()
    for k in range(4):
        grad_top[:, k] = all_t[k, 0:27].astype(F32)
    mstep_f.wait_send()
    mback_f.wait_recv()
    grad_mid[...] = all_m[0:27].astype(F32)


def fused_device(sizes, volume, kernel_mid, kernel_top, upstream):
    vol = jnp.transpose(volume[0], (1, 0, 2)).astype(F32)
    upper = jnp.transpose(upstream[0, :, :, 0, :], (1, 0, 2)).astype(F32).reshape(16, 128)
    vm = pltpu.VMEM
    block, mid, top = pl.pallas_call(
        functools.partial(fused_body, sizes),
        out_shape=(
            jax.ShapeDtypeStruct((16, 128), F32),
            jax.ShapeDtypeStruct((27, 32, 128), F32),
            jax.ShapeDtypeStruct((27, 4, 32, 128), F32),
        ),
        in_specs=[pl.BlockSpec(memory_space=pltpu.VMEM)] * 4,
        out_specs=[pl.BlockSpec(memory_space=pltpu.VMEM)] * 3,
        scratch_shapes=[
            vm((10, 32, 256), F32), vm((6, 32, 256), F32), vm((6, 32, 256), F32),
            vm((10, 16, 768), BF), vm((6, 16, 768), BF),
            vm((3, 768, 512), BF), vm((3, 256, 768), BF),
            vm((128, 512), F32), vm((64, 128), F32), vm((64, 128), F32),
            vm((4, 16, 256), F32), vm((4, 8, 256), F32),
            vm((28, 4, 32, 128), F32), vm((28, 2, 32, 128), BF), vm((28, 2, 32, 128), BF),
            vm((28, 32, 128), BF), vm((28, 32, 128), BF), vm((28, 2, 32, 128), F32),
            vm((28, 32, 128), BF), vm((3, 7, 32, 128), BF), vm((4, 28, 32, 128), BF),
            vm((2, 28, 32, 128), F32), vm((2, 14, 32, 128), BF), vm((2, 14, 32, 128), BF),
            vm((14, 32, 128), BF), vm((14, 32, 128), BF), vm((7, 32, 128), BF), vm((7, 32, 128), BF),
            vm((4, 7, 32, 128), BF), vm((28, 32, 128), BF),
            pltpu.SemaphoreType.DMA((40,)), pltpu.SemaphoreType.DMA((40,)),
        ],
        compiler_params=pltpu.CompilerParams(
            collective_id=0, has_side_effects=True, vmem_limit_bytes=48 * 1024 * 1024
        ),
        name="fused",
    )(vol, kernel_mid, kernel_top, upper)
    block_out = jnp.transpose(block.reshape(2, 8, 128), (1, 0, 2)).astype(BF)[None, :, :, None, :]
    return (block_out, mid.reshape(864, 128), top.reshape(27, 128, 128))


def solution(mesh):
    sizes = (mesh.shape["sample"], mesh.shape["spatial"], mesh.shape["channel"])

    def per_device(volume, kernel_mid, kernel_top, upstream):
        fits = (
            sizes == (4, 4, 2)
            and volume.shape == (1, 16, 8, 256)
            and kernel_mid.shape == (27, 64, 128)
            and kernel_top.shape == (27, 128, 128)
            and upstream.shape == (1, 8, 2, 1, 128)
        )
        if fits:
            return fused_device(sizes, volume, kernel_mid, kernel_top, upstream)
        return on_device(volume, kernel_mid, kernel_top, upstream)

    return jax.shard_map(
        per_device,
        mesh=mesh,
        in_specs=(
            P("sample", "channel", "spatial", None),
            P(),
            P(None, "channel", None),
            P("sample", None, "spatial", None, "channel"),
        ),
        out_specs=(
            P("sample", None, "spatial", None, "channel"),
            P("channel", None),
            P(None, "channel", None),
        ),
        check_vma=False,
    )
```

```python
import functools

import jax
import jax.numpy as jnp
from jax import lax
from jax.experimental import pallas as pl
from jax.experimental.pallas import tpu as pltpu
from jax.sharding import PartitionSpec as P


def extended(cells, sides, width):
    for axis, dim in sides:
        count = lax.axis_size(axis)
        ends = count - 1
        head = lax.slice_in_dim(cells, 0, width, axis=dim)
        tail = lax.slice_in_dim(cells, cells.shape[dim] - width, cells.shape[dim], axis=dim)
        cells = jnp.concatenate(
            [
                lax.ppermute(tail, axis, [(i, (i + 1) % count) for i in range(ends)]),
                cells,
                lax.ppermute(head, axis, [((i + 1) % count, i) for i in range(ends)]),
            ],
            axis=dim,
        )
    return cells


def slope(values):
    sig = jax.nn.sigmoid(values)
    return sig * (1.0 + values * (1.0 - sig))


def pool_mean(field):
    h_size, d_size, w_size, c_size = field.shape
    blocks = field.reshape(h_size // 2, 2, d_size // 2, 2, w_size // 2, 2, c_size)
    return jnp.mean(blocks, axis=(1, 3, 5))


def spread(field):
    h_size, d_size, w_size, c_size = field.shape
    wide = jnp.broadcast_to(
        field[:, None, :, None, :, None, :], (h_size, 2, d_size, 2, w_size, 2, c_size)
    )
    return wide.reshape(2 * h_size, 2 * d_size, 2 * w_size, c_size) * 0.125


def width_taps(padded, off_rows, off_depth, row_count, depth_count, width_count, order):
    parts = []
    for off_width in order:
        parts.append(
            padded[
                off_rows : off_rows + row_count,
                off_depth : off_depth + depth_count,
                off_width : off_width + width_count,
                :,
            ]
        )
    joined = jnp.concatenate(parts, axis=3)
    return joined.reshape(row_count * depth_count * width_count, joined.shape[3])


def convolve(padded, kernel, row_count, depth_count, width_count):
    running = jnp.zeros((row_count * depth_count * width_count, kernel.shape[2]), jnp.float32)
    for off_depth in range(3):
        for off_rows in range(3):
            base = 9 * off_depth + 3 * off_rows
            joined = width_taps(
                padded, off_rows, off_depth, row_count, depth_count, width_count, (0, 1, 2)
            )
            stacked = kernel[base : base + 3].reshape(3 * kernel.shape[1], kernel.shape[2])
            running = running + jnp.dot(joined, stacked, preferred_element_type=jnp.float32)
    return running.reshape(row_count, depth_count, width_count, kernel.shape[2])


def convolve_turned(padded, kernel, row_count, depth_count, width_count):
    filters_here = kernel.shape[1]
    running = jnp.zeros((row_count * depth_count * width_count, filters_here), jnp.float32)
    for off_depth in range(3):
        for off_rows in range(3):
            base = 9 * off_depth + 3 * off_rows
            joined = width_taps(
                padded, off_rows, off_depth, row_count, depth_count, width_count, (0, 1, 2)
            )
            stacked = jnp.transpose(kernel[base : base + 3], (0, 2, 1)).reshape(
                3 * kernel.shape[2], filters_here
            )
            running = running + jnp.dot(joined, stacked, preferred_element_type=jnp.float32)
    return running.reshape(row_count, depth_count, width_count, filters_here)


def kernel_grad(padded, grads, row_count, depth_count, width_count):
    flat = grads.reshape(row_count * depth_count * width_count, grads.shape[3])
    pieces = []
    for off_depth in range(3):
        for off_rows in range(3):
            joined = width_taps(
                padded, off_rows, off_depth, row_count, depth_count, width_count, (0, 1, 2)
            )
            pieces.append(
                lax.dot_general(
                    joined, flat, (((0,), (0,)), ((), ())), preferred_element_type=jnp.float32
                )
            )
    stacked = jnp.stack(pieces)
    return stacked.reshape(27, padded.shape[3], grads.shape[3])


def kernel_grad_flipped(padded, grads, row_count, depth_count, width_count):
    flat = grads.reshape(row_count * depth_count * width_count, grads.shape[3])
    channels = padded.shape[3]
    filters_here = grads.shape[3]
    pieces = []
    for off_depth in range(3):
        for off_rows in range(3):
            joined = width_taps(
                padded, off_rows, off_depth, row_count, depth_count, width_count, (0, 1, 2)
            )
            pieces.append(
                lax.dot_general(
                    flat, joined, (((0,), (0,)), ((), ())), preferred_element_type=jnp.float32
                )
            )
    stacked = jnp.stack(pieces).reshape(9, filters_here, 3, channels)
    return jnp.transpose(stacked, (0, 2, 1, 3)).reshape(27, filters_here, channels)


def depth_rim(field):
    return extended(field, (("spatial", 1),), 1)


def pad_sides(field):
    return jnp.pad(field, ((1, 1), (0, 0), (1, 1), (0, 0)))


def share_rows(partial_grad):
    return lax.psum_scatter(partial_grad, "channel", scatter_dimension=0, tiled=True)


def on_device(volume, kernel_mid, kernel_top, upstream):
    channel_in = kernel_mid.shape[1]
    channel_mid = kernel_mid.shape[2]
    row_count = volume.shape[1]
    depth_count = volume.shape[2]
    width_count = volume.shape[3] // channel_in
    cells = volume[0].reshape(row_count, depth_count, width_count, channel_in)
    rimmed = extended(cells, (("spatial", 1), ("channel", 0)), 1)
    padded = jnp.pad(rimmed, ((0, 0), (0, 0), (1, 1), (0, 0)))
    pre_mid = convolve(padded, kernel_mid, row_count, depth_count, width_count)
    pooled = pool_mean(jax.nn.silu(pre_mid)).astype(jnp.bfloat16)
    gathered = lax.all_gather(pooled, "channel", axis=0, tiled=True)
    tall_rows = gathered.shape[0]
    half_depth = depth_count // 2
    half_width = width_count // 2
    top_pad = pad_sides(depth_rim(gathered))
    pre_top = convolve_turned(top_pad, kernel_top, tall_rows, half_depth, half_width)
    block_out = pool_mean(jax.nn.silu(pre_top)).astype(jnp.bfloat16)[None]
    grad_pre_top = (spread(upstream[0].astype(jnp.float32)) * slope(pre_top)).astype(jnp.bfloat16)
    top_part = kernel_grad_flipped(top_pad, grad_pre_top, tall_rows, half_depth, half_width)
    grad_pad = pad_sides(depth_rim(grad_pre_top))
    filters_here = kernel_top.shape[1]
    channel_top = kernel_top.shape[2]
    running = jnp.zeros(
        (lax.axis_size("channel") * (row_count // 2) * half_depth * half_width, channel_top),
        jnp.float32,
    )
    for off_depth in range(3):
        for off_rows in range(3):
            base = 9 * off_depth + 3 * off_rows
            joined = width_taps(
                grad_pad,
                2 - off_rows,
                2 - off_depth,
                lax.axis_size("channel") * (row_count // 2),
                half_depth,
                half_width,
                (2, 1, 0),
            )
            flipped = kernel_top[base : base + 3].reshape(3 * filters_here, channel_top)
            running = running + jnp.dot(joined, flipped, preferred_element_type=jnp.float32)
    grad_pooled = lax.psum_scatter(
        running.reshape(
            lax.axis_size("channel") * (row_count // 2), half_depth, half_width, channel_top
        ),
        "channel",
        scatter_dimension=0,
        tiled=True,
    )
    grad_pre_mid = (spread(grad_pooled) * slope(pre_mid)).astype(jnp.bfloat16)
    mid_part = kernel_grad(padded, grad_pre_mid, row_count, depth_count, width_count).reshape(
        27 * channel_in, channel_mid
    )
    whole_mid, grad_top = lax.psum((mid_part, top_part), ("sample", "spatial"))
    grad_mid = share_rows(whole_mid)
    return (block_out, grad_mid, grad_top)


BF = jnp.bfloat16
F32 = jnp.float32


def fused_body(
    sizes, vol, kmid, ktop, upper, block_out, grad_mid, grad_top,
    vpad, ppad, gpad, xmid, xtop, wmid, wtop, pre, fold0, fold1, part, part_in,
    kmid_v, ktop_v, wsem,
    acc_t, ta_s, ta_r, keep_t, tb_s, tb_r, own_t, tc_s, tc_r, td_s, td_r, all_t,
    acc_m, ma_s, ma_r, mkeep, mb_s, mb_r, mc_s, mc_r, md_s, md_r, me_s, me_r, all_m,
    ssem, rsem,
):
    samples, slabs, chans = sizes
    b = lax.axis_index("sample")
    s = lax.axis_index("spatial")
    c = lax.axis_index("channel")
    core = lax.rem(s, 2)
    side = lax.div(s, 2)
    s_core = s + 1 - 2 * core
    s_side = s + 2 - 4 * side
    count = [0]

    def place(bb, ss, cc):
        return {"sample": bb, "spatial": ss, "channel": cc}

    def link(source, target, device):
        k = count[0]
        count[0] += 1
        return pltpu.make_async_remote_copy(
            src_ref=source, dst_ref=target, send_sem=ssem.at[k], recv_sem=rsem.at[k],
            device_id=device, device_id_type=pl.DeviceIdType.MESH,
        )

    fetch_mid = pltpu.make_async_copy(kmid, kmid_v, wsem.at[0])
    fetch_top = pltpu.make_async_copy(ktop, ktop_v, wsem.at[1])
    fetch_mid.start()
    fetch_top.start()
    vpad[...] = jnp.zeros_like(vpad)
    ppad[...] = jnp.zeros_like(ppad)
    gpad[...] = jnp.zeros_like(gpad)

    barrier = pltpu.get_barrier_semaphore()
    greeted = 0
    for ds in range(slabs):
        for dc in range(chans):
            if ds or dc:
                pl.semaphore_signal(
                    barrier, inc=1,
                    device_id=place(b, lax.rem(s + ds, slabs), lax.rem(c + dc, chans)),
                    device_id_type=pl.DeviceIdType.MESH,
                )
                greeted += 1
    for db in range(1, samples):
        pl.semaphore_signal(
            barrier, inc=1, device_id=place(lax.rem(b + db, samples), s, c),
            device_id_type=pl.DeviceIdType.MESH,
        )
        greeted += 1
    vpad[1:9, 8:24, :] = jnp.transpose(vol[...].astype(F32), (1, 0, 2))
    wmid[...] = jnp.zeros_like(wmid)
    pl.semaphore_wait(barrier, greeted)

    def inside(value, limit):
        return jnp.logical_and(value >= 0, value < limit)

    planes = {1: (slice(8, 9), slice(0, 1)), 0: (slice(1, 9), slice(1, 9)), -1: (slice(1, 2), slice(9, 10))}
    bands = {1: (slice(16, 24), slice(0, 8)), 0: (slice(8, 24), slice(8, 24)), -1: (slice(8, 16), slice(24, 32))}
    halo = []
    for ds in (0, 1, -1):
        for dc in (0, 1, -1):
            if ds == 0 and dc == 0:
                continue
            copy = link(
                vpad.at[planes[ds][0], bands[dc][0]], vpad.at[planes[ds][1], bands[dc][1]],
                place(b, lax.rem(s + ds + slabs, slabs), lax.rem(c + dc + chans, chans)),
            )
            out_ok = jnp.logical_and(inside(s + ds, slabs), inside(c + dc, chans))
            in_ok = jnp.logical_and(inside(s - ds, slabs), inside(c - dc, chans))
            halo.append((copy, out_ok, in_ok))
    for copy, out_ok, _ in halo:
        @pl.when(out_ok)
        def _(copy=copy):
            copy.start()

    fetch_mid.wait()
    fetch_top.wait()
    for i in range(3):
        for j in range(3):
            for xi in range(4):
                for xo in range(4):
                    l = xi - xo + 1
                    if 0 <= l <= 2:
                        wmid[i, j * 256 + xi * 64 : j * 256 + xi * 64 + 64, xo * 128 : xo * 128 + 128] = kmid_v[9 * i + 3 * j + l]
            for xi in range(2):
                for xo in range(2):
                    wtop[i, xo * 128 : xo * 128 + 128, j * 256 + xi * 128 : j * 256 + xi * 128 + 128] = ktop_v[9 * i + 3 * j + xi - xo + 1]
    acc_t[:, :, 27] = jnp.zeros((2, 4, 16, 128), F32)
    acc_m[:, :, 27] = jnp.zeros((2, 2, 16, 128), F32)

    for copy, out_ok, in_ok in halo:
        @pl.when(out_ok)
        def _(copy=copy):
            copy.wait_send()

        @pl.when(in_ok)
        def _(copy=copy):
            copy.wait_recv()

    for j in range(3):
        xmid[:, :, j * 256 : j * 256 + 256] = vpad[:, 7 + j : 23 + j, :].astype(BF)
    total = jnp.zeros((128, 512), F32)
    for i in range(3):
        total = total + jnp.dot(xmid[i : i + 8].reshape(128, 768), wmid[i], preferred_element_type=F32)
    pre[...] = total
    act = (total / (1.0 + jnp.exp(-total))).reshape(4, 2, 16, 512)
    act = act[:, 0] + act[:, 1]
    fold0[...] = (act[:, :, 0:128] + act[:, :, 128:256]).reshape(64, 128)
    fold1[...] = (act[:, :, 256:384] + act[:, :, 384:512]).reshape(64, 128)
    mine = pl.ds(pl.multiple_of(8 + 8 * c, 8), 8)
    for x, fold in enumerate((fold0, fold1)):
        pooled = (fold[pl.ds(0, 32, 2), :] + fold[pl.ds(1, 32, 2), :]) * 0.125
        ppad[1:5, mine, x * 128 : x * 128 + 128] = pooled.astype(BF).astype(F32).reshape(4, 8, 128)

    swaps = []
    for ds, take, put in ((0, slice(1, 5), slice(1, 5)), (1, slice(4, 5), slice(0, 1)), (-1, slice(1, 2), slice(5, 6))):
        for dc in range(chans):
            if ds == 0 and dc == 0:
                continue
            device = place(b, lax.rem(s + ds + slabs, slabs), lax.rem(c + dc, chans))
            theirs = pl.ds(pl.multiple_of(8 + 8 * lax.rem(c - dc + chans, chans), 8), 8)
            copy = link(ppad.at[take, mine], ppad.at[put, mine], device)
            count[0] -= 1
            back = link(ppad.at[take, theirs], ppad.at[put, theirs], device)
            swaps.append((copy, back, inside(s + ds, slabs), inside(s - ds, slabs)))
    for copy, _, out_ok, _ in swaps:
        @pl.when(out_ok)
        def _(copy=copy):
            copy.start()
    for copy, back, out_ok, in_ok in swaps:
        @pl.when(out_ok)
        def _(copy=copy):
            copy.wait_send()

        @pl.when(in_ok)
        def _(back=back):
            back.wait_recv()

    for j in range(3):
        xtop[:, :, j * 256 : j * 256 + 256] = ppad[:, 7 + j : 23 + j, :].astype(BF)
    top = jnp.zeros((64, 256), F32)
    for i in range(3):
        top = top + lax.dot_general(
            xtop[i : i + 4].reshape(64, 768), wtop[i], (((1,), (1,)), ((), ())), preferred_element_type=F32
        )
    sig = 1.0 / (1.0 + jnp.exp(-top))
    fold1[pl.ds(0, 16, 2), :] = upper[...]
    fold1[pl.ds(1, 16, 2), :] = upper[...]
    wide = fold1[0:32, :].reshape(2, 1, 16, 128)
    wide = jnp.broadcast_to(wide, (2, 2, 16, 128)).reshape(64, 128)
    wide = jnp.concatenate([wide, wide], axis=1) * 0.125
    grads = wide * (sig * (1.0 + top * (1.0 - sig)))
    grads_bf = grads.astype(BF)
    gpad[1:5, 8:24, :] = grads_bf.astype(F32).reshape(4, 16, 256)
    rims = []
    for ds, take, put in ((1, slice(4, 5), slice(0, 1)), (-1, slice(1, 2), slice(5, 6))):
        copy = link(gpad.at[take, 8:24], gpad.at[put, 8:24], place(b, lax.rem(s + ds + slabs, slabs), c))
        rims.append((copy, inside(s + ds, slabs), inside(s - ds, slabs)))
    for copy, out_ok, _ in rims:
        @pl.when(out_ok)
        def _(copy=copy):
            copy.start()
    act = (top / (1.0 + jnp.exp(-top))).reshape(2, 2, 16, 256)
    act = act[:, 0] + act[:, 1]
    fold0[0:32, :] = (act[:, :, 0:128] + act[:, :, 128:256]).reshape(32, 128)
    block_out[...] = (fold0[pl.ds(0, 16, 2), :] + fold0[pl.ds(1, 16, 2), :]) * 0.125

    def put_top(tap, block):
        for q in range(4):
            for p in range(2):
                acc_t[p, q, tap] = block[32 * q + 16 * p : 32 * q + 16 * p + 16]

    for i in range(3):
        for j in range(3):
            cross = lax.dot_general(
                grads_bf, xtop[i : i + 4, :, j * 256 : j * 256 + 256].reshape(64, 256),
                (((0,), (0,)), ((), ())), preferred_element_type=F32,
            )
            tap = 9 * i + 3 * j
            put_top(tap, cross[128:256, 0:128])
            put_top(tap + 1, cross[0:128, 0:128] + cross[128:256, 128:256])
            put_top(tap + 2, cross[0:128, 128:256])

    zb = lax.rem(b, 2)
    zh = lax.div(b, 2)
    to_core = place(b, s_core, c)
    to_side = place(b, s_side, c)
    to_z1 = place(b + 1 - 2 * zb, s, c)
    to_z2 = place(b + 2 - 4 * zh, s, c)
    other = 1 - c
    to_chan = place(b, s, other)
    quarter = 2 * core + side
    mirror = 2 * core + 1 - side

    def share(pick, device):
        near, far = pick
        copy = link(near, near, device)
        count[0] -= 1
        back = link(far, far, device)
        copy.start()
        return copy, back

    def settle(pair):
        pair[0].wait_send()
        pair[1].wait_recv()

    def top_chain(p):
        ta_s[p] = acc_t[p, pl.ds(2 * (1 - core), 2)].astype(BF)
        step = link(ta_s.at[p], ta_r.at[p], to_core)
        step.start()
        yield
        step.wait()
        keep_t[p] = acc_t[p, pl.ds(2 * core, 2)] + ta_r[p].astype(F32)
        tb_s[p] = keep_t[p, 1 - side].astype(BF)
        step = link(tb_s.at[p], tb_r.at[p], to_side)
        step.start()
        yield
        step.wait()
        own_t[p] = (keep_t[p, side] + tb_r[p].astype(F32)).reshape(2, 2, 7, 16, 128)
        tc_s[p] = own_t[p, :, 1 - zb].astype(BF)
        step = link(tc_s.at[p], tc_r.at[p], to_z1)
        step.start()
        yield
        step.wait()
        td_s[p] = (own_t[p, 1 - zh, zb] + tc_r[p, 1 - zh].astype(F32)).astype(BF)
        step = link(td_s.at[p], td_r.at[p], to_z2)
        step.start()
        kept = own_t[p, zh, zb] + tc_r[p, zh].astype(F32)
        yield
        step.wait()
        all_t[p, quarter, zh, zb] = (kept + td_r[p].astype(F32)).astype(BF)
        pair = share((all_t.at[p, quarter, zh, zb], all_t.at[p, quarter, 1 - zh, zb]), to_z2)
        yield
        settle(pair)
        pair = share((all_t.at[p, quarter, :, zb], all_t.at[p, quarter, :, 1 - zb]), to_z1)
        yield
        settle(pair)
        pair = share((all_t.at[p, quarter], all_t.at[p, mirror]), to_side)
        yield
        settle(pair)
        pair = share((all_t.at[p, pl.ds(2 * core, 2)], all_t.at[p, pl.ds(2 * (1 - core), 2)]), to_core)
        yield
        settle(pair)
        for q in range(4):
            grad_top[:, q, 16 * p : 16 * p + 16] = all_t[p, q].reshape(28, 16, 128)[0:27].astype(F32)
        yield

    def mid_chain(p):
        ma_s[p] = acc_m[p, :, pl.ds(14 * (1 - core), 14)].astype(BF)
        step = link(ma_s.at[p], ma_r.at[p], to_core)
        step.start()
        yield
        step.wait()
        mb_s[p] = (acc_m[p, other, pl.ds(14 * core, 14)] + ma_r[p, other].astype(F32)).astype(BF)
        step = link(mb_s.at[p], mb_r.at[p], to_chan)
        step.start()
        mkeep[p] = acc_m[p, c, pl.ds(14 * core, 14)] + ma_r[p, c].astype(F32)
        yield
        step.wait()
        near, far = pl.ds(7 * side, 7), pl.ds(7 * (1 - side), 7)
        mc_s[p] = (mkeep[p, far] + mb_r[p, far].astype(F32)).astype(BF)
        step = link(mc_s.at[p], mc_r.at[p], to_side)
        step.start()
        held = mkeep[p, near] + mb_r[p, near].astype(F32)
        yield
        step.wait()
        md_s[p] = (held + mc_r[p].astype(F32)).astype(BF)
        step = link(md_s.at[p], md_r.at[p], to_z1)
        step.start()
        yield
        step.wait()
        me_s[p] = (md_s[p].astype(F32) + md_r[p].astype(F32)).astype(BF)
        step = link(me_s.at[p], me_r.at[p], to_z2)
        step.start()
        yield
        step.wait()
        all_m[p, quarter] = (me_s[p].astype(F32) + me_r[p].astype(F32)).astype(BF)
        pair = share((all_m.at[p, quarter], all_m.at[p, mirror]), to_side)
        yield
        settle(pair)
        pair = share((all_m.at[p, pl.ds(2 * core, 2)], all_m.at[p, pl.ds(2 * (1 - core), 2)]), to_core)
        yield
        settle(pair)
        grad_mid[:, 16 * p : 16 * p + 16] = all_m[p].reshape(28, 16, 128)[0:27].astype(F32)
        yield

    chains = {"t": top_chain(0), "u": top_chain(1), "m": mid_chain(0), "n": mid_chain(1)}

    def advance(names):
        for name in names:
            next(chains[name])

    advance("tu")

    for copy, out_ok, in_ok in rims:
        @pl.when(out_ok)
        def _(copy=copy):
            copy.wait_send()

        @pl.when(in_ok)
        def _(copy=copy):
            copy.wait_recv()
    back_sum = jnp.zeros((64, 256), F32)
    for j in range(3):
        lined = gpad[:, 9 - j : 25 - j, :].astype(BF)
        for i in range(3):
            back_sum = back_sum + jnp.dot(
                lined[2 - i : 6 - i].reshape(64, 256), wtop[i, :, j * 256 : j * 256 + 256], preferred_element_type=F32
            )
    part[...] = back_sum.reshape(4, 16, 256)
    give = link(part.at[:, pl.ds(pl.multiple_of(8 * other, 8), 8)], part_in, to_chan)
    give.start()
    advance("tu")
    field = pre[...]
    sig = 1.0 / (1.0 + jnp.exp(-field))
    pre[...] = 0.125 * (sig * (1.0 + field * (1.0 - sig)))

    give.wait()
    pooled_grad = part[:, pl.ds(pl.multiple_of(8 * c, 8), 8)] + part_in[...]
    wides = []
    for x, fold in enumerate((fold0, fold1)):
        half = pooled_grad[:, :, x * 128 : x * 128 + 128].reshape(32, 128)
        fold[pl.ds(0, 32, 2), :] = half
        fold[pl.ds(1, 32, 2), :] = half
        half = jnp.broadcast_to(fold[...].reshape(4, 1, 16, 128), (4, 2, 16, 128)).reshape(128, 128)
        wides += [half, half]
    grads_mid = (jnp.concatenate(wides, axis=1) * pre[...]).astype(BF)

    def mid_taps(i):
        for j in range(3):
            cross = lax.dot_general(
                xmid[i : i + 8, :, j * 256 : j * 256 + 256].reshape(128, 256), grads_mid,
                (((0,), (0,)), ((), ())), preferred_element_type=F32,
            )
            for l in range(3):
                block = None
                for xo in range(4):
                    xi = xo + l - 1
                    if 0 <= xi < 4:
                        term = cross[xi * 64 : xi * 64 + 64, xo * 128 : xo * 128 + 128]
                        block = term if block is None else block + term
                for n in range(2):
                    unit = 2 * (9 * i + 3 * j + l) + n
                    for p in range(2):
                        acc_m[p, unit // 27, unit % 27] = block[32 * n + 16 * p : 32 * n + 16 * p + 16]

    mid_taps(0)
    mid_taps(1)
    advance("t")
    mid_taps(2)
    advance("mnumtnumtnumtnumtnumtnumntumn")


def fused_device(sizes, volume, kernel_mid, kernel_top, upstream):
    vol = volume[0]
    upper = jnp.transpose(upstream[0, :, :, 0, :], (1, 0, 2)).astype(F32).reshape(16, 128)
    vm = pltpu.VMEM
    block, mid, top = pl.pallas_call(
        functools.partial(fused_body, sizes),
        out_shape=(
            jax.ShapeDtypeStruct((16, 128), F32),
            jax.ShapeDtypeStruct((27, 32, 128), F32),
            jax.ShapeDtypeStruct((27, 4, 32, 128), F32),
        ),
        in_specs=[
            pl.BlockSpec(memory_space=pltpu.VMEM),
            pl.BlockSpec(memory_space=pltpu.HBM),
            pl.BlockSpec(memory_space=pltpu.HBM),
            pl.BlockSpec(memory_space=pltpu.VMEM),
        ],
        out_specs=[pl.BlockSpec(memory_space=pltpu.VMEM)] * 3,
        scratch_shapes=[
            vm((10, 32, 256), F32), vm((6, 32, 256), F32), vm((6, 32, 256), F32),
            vm((10, 16, 768), BF), vm((6, 16, 768), BF),
            vm((3, 768, 512), BF), vm((3, 256, 768), BF),
            vm((128, 512), F32), vm((64, 128), F32), vm((64, 128), F32),
            vm((4, 16, 256), F32), vm((4, 8, 256), F32),
            vm((27, 64, 128), BF), vm((27, 128, 128), BF), pltpu.SemaphoreType.DMA((2,)),
            vm((2, 4, 28, 16, 128), F32),
            vm((2, 2, 28, 16, 128), BF), vm((2, 2, 28, 16, 128), BF), vm((2, 2, 28, 16, 128), F32),
            vm((2, 28, 16, 128), BF), vm((2, 28, 16, 128), BF), vm((2, 2, 2, 7, 16, 128), F32),
            vm((2, 2, 7, 16, 128), BF), vm((2, 2, 7, 16, 128), BF),
            vm((2, 7, 16, 128), BF), vm((2, 7, 16, 128), BF), vm((2, 4, 2, 2, 7, 16, 128), BF),
            vm((2, 2, 28, 16, 128), F32),
            vm((2, 2, 14, 16, 128), BF), vm((2, 2, 14, 16, 128), BF), vm((2, 14, 16, 128), F32),
            vm((2, 14, 16, 128), BF), vm((2, 14, 16, 128), BF),
            vm((2, 7, 16, 128), BF), vm((2, 7, 16, 128), BF), vm((2, 7, 16, 128), BF), vm((2, 7, 16, 128), BF),
            vm((2, 7, 16, 128), BF), vm((2, 7, 16, 128), BF), vm((2, 4, 7, 16, 128), BF),
            pltpu.SemaphoreType.DMA((64,)), pltpu.SemaphoreType.DMA((64,)),
        ],
        compiler_params=pltpu.CompilerParams(
            collective_id=0, has_side_effects=True, vmem_limit_bytes=40 * 1024 * 1024
        ),
        name="fused",
    )(vol, kernel_mid, kernel_top, upper)
    block_out = jnp.transpose(block.reshape(2, 8, 128), (1, 0, 2)).astype(BF)[None, :, :, None, :]
    return (block_out, mid.reshape(864, 128), top.reshape(27, 128, 128))


def solution(mesh):
    sizes = (mesh.shape["sample"], mesh.shape["spatial"], mesh.shape["channel"])

    def per_device(volume, kernel_mid, kernel_top, upstream):
        fits = (
            sizes == (4, 4, 2)
            and volume.shape == (1, 16, 8, 256)
            and kernel_mid.shape == (27, 64, 128)
            and kernel_top.shape == (27, 128, 128)
            and upstream.shape == (1, 8, 2, 1, 128)
        )
        if fits:
            return fused_device(sizes, volume, kernel_mid, kernel_top, upstream)
        return on_device(volume, kernel_mid, kernel_top, upstream)

    return jax.shard_map(
        per_device,
        mesh=mesh,
        in_specs=(
            P("sample", "channel", "spatial", None),
            P(),
            P(None, "channel", None),
            P("sample", None, "spatial", None, "channel"),
        ),
        out_specs=(
            P("sample", None, "spatial", None, "channel"),
            P("channel", None),
            P(None, "channel", None),
        ),
        check_vma=False,
    )
```

```python
import functools

import jax
import jax.numpy as jnp
from jax import lax
from jax.experimental import pallas as pl
from jax.experimental.pallas import tpu as pltpu
from jax.sharding import PartitionSpec as P


def extended(cells, sides, width):
    for axis, dim in sides:
        count = lax.axis_size(axis)
        ends = count - 1
        head = lax.slice_in_dim(cells, 0, width, axis=dim)
        tail = lax.slice_in_dim(cells, cells.shape[dim] - width, cells.shape[dim], axis=dim)
        cells = jnp.concatenate(
            [
                lax.ppermute(tail, axis, [(i, (i + 1) % count) for i in range(ends)]),
                cells,
                lax.ppermute(head, axis, [((i + 1) % count, i) for i in range(ends)]),
            ],
            axis=dim,
        )
    return cells


def slope(values):
    sig = jax.nn.sigmoid(values)
    return sig * (1.0 + values * (1.0 - sig))


def pool_mean(field):
    h_size, d_size, w_size, c_size = field.shape
    blocks = field.reshape(h_size // 2, 2, d_size // 2, 2, w_size // 2, 2, c_size)
    return jnp.mean(blocks, axis=(1, 3, 5))


def spread(field):
    h_size, d_size, w_size, c_size = field.shape
    wide = jnp.broadcast_to(
        field[:, None, :, None, :, None, :], (h_size, 2, d_size, 2, w_size, 2, c_size)
    )
    return wide.reshape(2 * h_size, 2 * d_size, 2 * w_size, c_size) * 0.125


def width_taps(padded, off_rows, off_depth, row_count, depth_count, width_count, order):
    parts = []
    for off_width in order:
        parts.append(
            padded[
                off_rows : off_rows + row_count,
                off_depth : off_depth + depth_count,
                off_width : off_width + width_count,
                :,
            ]
        )
    joined = jnp.concatenate(parts, axis=3)
    return joined.reshape(row_count * depth_count * width_count, joined.shape[3])


def convolve(padded, kernel, row_count, depth_count, width_count):
    running = jnp.zeros((row_count * depth_count * width_count, kernel.shape[2]), jnp.float32)
    for off_depth in range(3):
        for off_rows in range(3):
            base = 9 * off_depth + 3 * off_rows
            joined = width_taps(
                padded, off_rows, off_depth, row_count, depth_count, width_count, (0, 1, 2)
            )
            stacked = kernel[base : base + 3].reshape(3 * kernel.shape[1], kernel.shape[2])
            running = running + jnp.dot(joined, stacked, preferred_element_type=jnp.float32)
    return running.reshape(row_count, depth_count, width_count, kernel.shape[2])


def convolve_turned(padded, kernel, row_count, depth_count, width_count):
    filters_here = kernel.shape[1]
    running = jnp.zeros((row_count * depth_count * width_count, filters_here), jnp.float32)
    for off_depth in range(3):
        for off_rows in range(3):
            base = 9 * off_depth + 3 * off_rows
            joined = width_taps(
                padded, off_rows, off_depth, row_count, depth_count, width_count, (0, 1, 2)
            )
            stacked = jnp.transpose(kernel[base : base + 3], (0, 2, 1)).reshape(
                3 * kernel.shape[2], filters_here
            )
            running = running + jnp.dot(joined, stacked, preferred_element_type=jnp.float32)
    return running.reshape(row_count, depth_count, width_count, filters_here)


def kernel_grad(padded, grads, row_count, depth_count, width_count):
    flat = grads.reshape(row_count * depth_count * width_count, grads.shape[3])
    pieces = []
    for off_depth in range(3):
        for off_rows in range(3):
            joined = width_taps(
                padded, off_rows, off_depth, row_count, depth_count, width_count, (0, 1, 2)
            )
            pieces.append(
                lax.dot_general(
                    joined, flat, (((0,), (0,)), ((), ())), preferred_element_type=jnp.float32
                )
            )
    stacked = jnp.stack(pieces)
    return stacked.reshape(27, padded.shape[3], grads.shape[3])


def kernel_grad_flipped(padded, grads, row_count, depth_count, width_count):
    flat = grads.reshape(row_count * depth_count * width_count, grads.shape[3])
    channels = padded.shape[3]
    filters_here = grads.shape[3]
    pieces = []
    for off_depth in range(3):
        for off_rows in range(3):
            joined = width_taps(
                padded, off_rows, off_depth, row_count, depth_count, width_count, (0, 1, 2)
            )
            pieces.append(
                lax.dot_general(
                    flat, joined, (((0,), (0,)), ((), ())), preferred_element_type=jnp.float32
                )
            )
    stacked = jnp.stack(pieces).reshape(9, filters_here, 3, channels)
    return jnp.transpose(stacked, (0, 2, 1, 3)).reshape(27, filters_here, channels)


def depth_rim(field):
    return extended(field, (("spatial", 1),), 1)


def pad_sides(field):
    return jnp.pad(field, ((1, 1), (0, 0), (1, 1), (0, 0)))


def share_rows(partial_grad):
    return lax.psum_scatter(partial_grad, "channel", scatter_dimension=0, tiled=True)


def on_device(volume, kernel_mid, kernel_top, upstream):
    channel_in = kernel_mid.shape[1]
    channel_mid = kernel_mid.shape[2]
    row_count = volume.shape[1]
    depth_count = volume.shape[2]
    width_count = volume.shape[3] // channel_in
    cells = volume[0].reshape(row_count, depth_count, width_count, channel_in)
    rimmed = extended(cells, (("spatial", 1), ("channel", 0)), 1)
    padded = jnp.pad(rimmed, ((0, 0), (0, 0), (1, 1), (0, 0)))
    pre_mid = convolve(padded, kernel_mid, row_count, depth_count, width_count)
    pooled = pool_mean(jax.nn.silu(pre_mid)).astype(jnp.bfloat16)
    gathered = lax.all_gather(pooled, "channel", axis=0, tiled=True)
    tall_rows = gathered.shape[0]
    half_depth = depth_count // 2
    half_width = width_count // 2
    top_pad = pad_sides(depth_rim(gathered))
    pre_top = convolve_turned(top_pad, kernel_top, tall_rows, half_depth, half_width)
    block_out = pool_mean(jax.nn.silu(pre_top)).astype(jnp.bfloat16)[None]
    grad_pre_top = (spread(upstream[0].astype(jnp.float32)) * slope(pre_top)).astype(jnp.bfloat16)
    top_part = kernel_grad_flipped(top_pad, grad_pre_top, tall_rows, half_depth, half_width)
    grad_pad = pad_sides(depth_rim(grad_pre_top))
    filters_here = kernel_top.shape[1]
    channel_top = kernel_top.shape[2]
    running = jnp.zeros(
        (lax.axis_size("channel") * (row_count // 2) * half_depth * half_width, channel_top),
        jnp.float32,
    )
    for off_depth in range(3):
        for off_rows in range(3):
            base = 9 * off_depth + 3 * off_rows
            joined = width_taps(
                grad_pad,
                2 - off_rows,
                2 - off_depth,
                lax.axis_size("channel") * (row_count // 2),
                half_depth,
                half_width,
                (2, 1, 0),
            )
            flipped = kernel_top[base : base + 3].reshape(3 * filters_here, channel_top)
            running = running + jnp.dot(joined, flipped, preferred_element_type=jnp.float32)
    grad_pooled = lax.psum_scatter(
        running.reshape(
            lax.axis_size("channel") * (row_count // 2), half_depth, half_width, channel_top
        ),
        "channel",
        scatter_dimension=0,
        tiled=True,
    )
    grad_pre_mid = (spread(grad_pooled) * slope(pre_mid)).astype(jnp.bfloat16)
    mid_part = kernel_grad(padded, grad_pre_mid, row_count, depth_count, width_count).reshape(
        27 * channel_in, channel_mid
    )
    whole_mid, grad_top = lax.psum((mid_part, top_part), ("sample", "spatial"))
    grad_mid = share_rows(whole_mid)
    return (block_out, grad_mid, grad_top)


BF = jnp.bfloat16
F32 = jnp.float32


def fused_body(
    sizes, vol, kmid, ktop, upper, block_out, grad_mid, grad_top,
    vpad, pbuf, gall, gturn, xfull, ppad, gpad, xmid, xtop, wmid, wtop, pre, fold0, fold1, part, part_in,
    kmid_v, ktop_v, wsem,
    own_t, tc_s, tc_r, td_s, td_r, all_t,
    acc_m, ma_s, ma_r, mkeep, mb_s, mb_r, mc_s, mc_r, md_s, md_r, me_s, me_r, all_m,
    ssem, rsem,
):
    samples, slabs, chans = sizes
    b = lax.axis_index("sample")
    s = lax.axis_index("spatial")
    c = lax.axis_index("channel")
    core = lax.rem(s, 2)
    side = lax.div(s, 2)
    s_core = s + 1 - 2 * core
    s_side = s + 2 - 4 * side
    count = [0]

    def place(bb, ss, cc):
        return {"sample": bb, "spatial": ss, "channel": cc}

    def link(source, target, device):
        k = count[0]
        count[0] += 1
        return pltpu.make_async_remote_copy(
            src_ref=source, dst_ref=target, send_sem=ssem.at[k], recv_sem=rsem.at[k],
            device_id=device, device_id_type=pl.DeviceIdType.MESH,
        )

    fetch_mid = pltpu.make_async_copy(kmid, kmid_v, wsem.at[0])
    fetch_top = pltpu.make_async_copy(ktop, ktop_v, wsem.at[1])
    fetch_mid.start()
    fetch_top.start()
    vpad[...] = jnp.zeros_like(vpad)
    ppad[...] = jnp.zeros_like(ppad)
    pbuf[...] = jnp.zeros_like(pbuf)
    gall[...] = jnp.zeros_like(gall)
    gpad[...] = jnp.zeros_like(gpad)

    barrier = pltpu.get_barrier_semaphore()
    greeted = 0
    for ds in range(slabs):
        for dc in range(chans):
            if ds or dc:
                pl.semaphore_signal(
                    barrier, inc=1,
                    device_id=place(b, lax.rem(s + ds, slabs), lax.rem(c + dc, chans)),
                    device_id_type=pl.DeviceIdType.MESH,
                )
                greeted += 1
    for db in range(1, samples):
        pl.semaphore_signal(
            barrier, inc=1, device_id=place(lax.rem(b + db, samples), s, c),
            device_id_type=pl.DeviceIdType.MESH,
        )
        greeted += 1
    vpad[1:9, 8:24, :] = jnp.transpose(vol[...].astype(F32), (1, 0, 2))
    wmid[...] = jnp.zeros_like(wmid)
    pl.semaphore_wait(barrier, greeted)

    def inside(value, limit):
        return jnp.logical_and(value >= 0, value < limit)

    planes = {1: (slice(8, 9), slice(0, 1)), 0: (slice(1, 9), slice(1, 9)), -1: (slice(1, 2), slice(9, 10))}
    bands = {1: (slice(16, 24), slice(0, 8)), 0: (slice(8, 24), slice(8, 24)), -1: (slice(8, 16), slice(24, 32))}
    halo = []
    for ds in (0, 1, -1):
        for dc in (0, 1, -1):
            if ds == 0 and dc == 0:
                continue
            copy = link(
                vpad.at[planes[ds][0], bands[dc][0]], vpad.at[planes[ds][1], bands[dc][1]],
                place(b, lax.rem(s + ds + slabs, slabs), lax.rem(c + dc + chans, chans)),
            )
            out_ok = jnp.logical_and(inside(s + ds, slabs), inside(c + dc, chans))
            in_ok = jnp.logical_and(inside(s - ds, slabs), inside(c - dc, chans))
            halo.append((copy, out_ok, in_ok))
    for copy, out_ok, _ in halo:
        @pl.when(out_ok)
        def _(copy=copy):
            copy.start()

    fetch_mid.wait()
    fetch_top.wait()
    for i in range(3):
        for j in range(3):
            for xi in range(4):
                for xo in range(4):
                    l = xi - xo + 1
                    if 0 <= l <= 2:
                        wmid[i, j * 256 + xi * 64 : j * 256 + xi * 64 + 64, xo * 128 : xo * 128 + 128] = kmid_v[9 * i + 3 * j + l]
            for xi in range(2):
                for xo in range(2):
                    wtop[i, xo * 128 : xo * 128 + 128, j * 256 + xi * 128 : j * 256 + xi * 128 + 128] = ktop_v[9 * i + 3 * j + xi - xo + 1]
    own_t[:, 1, 1, 6] = jnp.zeros((2, 16, 128), F32)
    acc_m[:, :, 27] = jnp.zeros((2, 2, 16, 128), F32)

    for copy, out_ok, in_ok in halo:
        @pl.when(out_ok)
        def _(copy=copy):
            copy.wait_send()

        @pl.when(in_ok)
        def _(copy=copy):
            copy.wait_recv()

    for j in range(3):
        xmid[:, :, j * 256 : j * 256 + 256] = vpad[:, 7 + j : 23 + j, :].astype(BF)
    total = jnp.zeros((128, 512), F32)
    for i in range(3):
        total = total + jnp.dot(xmid[i : i + 8].reshape(128, 768), wmid[i], preferred_element_type=F32)
    pre[...] = total
    act = (total / (1.0 + jnp.exp(-total))).reshape(4, 2, 16, 512)
    act = act[:, 0] + act[:, 1]
    fold0[...] = (act[:, :, 0:128] + act[:, :, 128:256]).reshape(64, 128)
    fold1[...] = (act[:, :, 256:384] + act[:, :, 384:512]).reshape(64, 128)
    slab = pl.ds(1 + 4 * s, 4)
    nearby = pl.ds(4 * s, 6)
    for x, fold in enumerate((fold0, fold1)):
        pooled = (fold[pl.ds(0, 32, 2), :] + fold[pl.ds(1, 32, 2), :]) * 0.125
        pbuf[slab, c, :, x * 128 : x * 128 + 128] = pooled.reshape(4, 8, 128).astype(BF)

    def pass_on(ref, ds, dc):
        device = place(b, lax.rem(s + ds, slabs), lax.rem(c + dc, chans))
        sender = pl.ds(1 + 4 * lax.rem(s - ds + slabs, slabs), 4)
        near, far = ref.at[slab, c], ref.at[sender, lax.rem(c - dc + chans, chans)]
        copy = link(near, near, device)
        count[0] -= 1
        back = link(far, far, device)
        copy.start()
        return copy, back

    def settle(pair):
        pair[0].wait_send()
        pair[1].wait_recv()

    soon = []
    late = []
    for ds in (0, 1, 3, 2):
        for dc in range(chans):
            if ds or dc:
                (late if ds == 2 else soon).append(pass_on(pbuf, ds, dc))
    for pair in soon:
        settle(pair)

    for cc in range(chans):
        ppad[nearby, 8 + 8 * cc : 16 + 8 * cc, :] = pbuf[nearby, cc].astype(F32)
    for j in range(3):
        xtop[:, :, j * 256 : j * 256 + 256] = ppad[nearby, 7 + j : 23 + j, :].astype(BF)
    top = jnp.zeros((64, 256), F32)
    for i in range(3):
        top = top + lax.dot_general(
            xtop[i : i + 4].reshape(64, 768), wtop[i], (((1,), (1,)), ((), ())), preferred_element_type=F32
        )
    sig = 1.0 / (1.0 + jnp.exp(-top))
    fold1[pl.ds(0, 16, 2), :] = upper[...]
    fold1[pl.ds(1, 16, 2), :] = upper[...]
    wide = fold1[0:32, :].reshape(2, 1, 16, 128)
    wide = jnp.broadcast_to(wide, (2, 2, 16, 128)).reshape(64, 128)
    wide = jnp.concatenate([wide, wide], axis=1) * 0.125
    grads = wide * (sig * (1.0 + top * (1.0 - sig)))
    grads_bf = grads.astype(BF)
    gall[slab] = grads_bf.reshape(4, 16, 256)
    rims = []
    for ds in (1, 3, 2):
        copy = link(gall.at[slab], gall.at[slab], place(b, lax.rem(s + ds, slabs), c))
        count[0] -= 1
        sender = pl.ds(1 + 4 * lax.rem(s - ds + slabs, slabs), 4)
        rims.append((copy, link(gall.at[sender], gall.at[sender], place(b, lax.rem(s + ds, slabs), c))))
        copy.start()
    act = (top / (1.0 + jnp.exp(-top))).reshape(2, 2, 16, 256)
    act = act[:, 0] + act[:, 1]
    fold0[0:32, :] = (act[:, :, 0:128] + act[:, :, 128:256]).reshape(32, 128)
    block_out[...] = (fold0[pl.ds(0, 16, 2), :] + fold0[pl.ds(1, 16, 2), :]) * 0.125

    zb = lax.rem(b, 2)
    zh = lax.div(b, 2)
    to_core = place(b, s_core, c)
    to_side = place(b, s_side, c)
    to_z1 = place(b + 1 - 2 * zb, s, c)
    to_z2 = place(b + 2 - 4 * zh, s, c)
    other = 1 - c
    to_chan = place(b, s, other)
    quarter = 2 * core + side
    mirror = 2 * core + 1 - side

    def share(pick, device):
        near, far = pick
        copy = link(near, near, device)
        count[0] -= 1
        back = link(far, far, device)
        copy.start()
        return copy, back

    def top_chain(p):
        tc_s[p] = own_t[p, :, 1 - zb].astype(BF)
        step = link(tc_s.at[p], tc_r.at[p], to_z1)
        step.start()
        yield
        step.wait()
        td_s[p] = (own_t[p, 1 - zh, zb] + tc_r[p, 1 - zh].astype(F32)).astype(BF)
        step = link(td_s.at[p], td_r.at[p], to_z2)
        step.start()
        kept = own_t[p, zh, zb] + tc_r[p, zh].astype(F32)
        yield
        step.wait()
        all_t[p, quarter, zh, zb] = (kept + td_r[p].astype(F32)).astype(BF)
        pair = share((all_t.at[p, quarter, zh, zb], all_t.at[p, quarter, 1 - zh, zb]), to_z2)
        yield
        settle(pair)
        pair = share((all_t.at[p, quarter, :, zb], all_t.at[p, quarter, :, 1 - zb]), to_z1)
        yield
        settle(pair)
        pair = share((all_t.at[p, quarter], all_t.at[p, mirror]), to_side)
        yield
        settle(pair)
        pair = share((all_t.at[p, pl.ds(2 * core, 2)], all_t.at[p, pl.ds(2 * (1 - core), 2)]), to_core)
        yield
        settle(pair)
        for q in range(4):
            grad_top[:, q, 16 * p : 16 * p + 16] = all_t[p, q].reshape(28, 16, 128)[0:27].astype(F32)
        yield

    def mid_chain(p):
        ma_s[p] = acc_m[p, :, pl.ds(14 * (1 - core), 14)].astype(BF)
        step = link(ma_s.at[p], ma_r.at[p], to_core)
        step.start()
        yield
        step.wait()
        mb_s[p] = (acc_m[p, other, pl.ds(14 * core, 14)] + ma_r[p, other].astype(F32)).astype(BF)
        step = link(mb_s.at[p], mb_r.at[p], to_chan)
        step.start()
        mkeep[p] = acc_m[p, c, pl.ds(14 * core, 14)] + ma_r[p, c].astype(F32)
        yield
        step.wait()
        near, far = pl.ds(7 * side, 7), pl.ds(7 * (1 - side), 7)
        mc_s[p] = (mkeep[p, far] + mb_r[p, far].astype(F32)).astype(BF)
        step = link(mc_s.at[p], mc_r.at[p], to_side)
        step.start()
        held = mkeep[p, near] + mb_r[p, near].astype(F32)
        yield
        step.wait()
        md_s[p] = (held + mc_r[p].astype(F32)).astype(BF)
        step = link(md_s.at[p], md_r.at[p], to_z1)
        step.start()
        yield
        step.wait()
        me_s[p] = (md_s[p].astype(F32) + md_r[p].astype(F32)).astype(BF)
        step = link(me_s.at[p], me_r.at[p], to_z2)
        step.start()
        yield
        step.wait()
        all_m[p, quarter] = (me_s[p].astype(F32) + me_r[p].astype(F32)).astype(BF)
        pair = share((all_m.at[p, quarter], all_m.at[p, mirror]), to_side)
        yield
        settle(pair)
        pair = share((all_m.at[p, pl.ds(2 * core, 2)], all_m.at[p, pl.ds(2 * (1 - core), 2)]), to_core)
        yield
        settle(pair)
        grad_mid[:, 16 * p : 16 * p + 16] = all_m[p].reshape(28, 16, 128)[0:27].astype(F32)
        yield

    chains = {"t": top_chain(0), "u": top_chain(1), "m": mid_chain(0), "n": mid_chain(1)}

    def advance(names):
        for name in names:
            next(chains[name])

    settle(rims[0])
    settle(rims[1])
    gpad[:, 8:24, :] = gall[nearby].astype(F32)
    back_sum = jnp.zeros((64, 256), F32)
    for j in range(3):
        lined = gpad[:, 9 - j : 25 - j, :].astype(BF)
        for i in range(3):
            back_sum = back_sum + jnp.dot(
                lined[2 - i : 6 - i].reshape(64, 256), wtop[i, :, j * 256 : j * 256 + 256], preferred_element_type=F32
            )
    part[...] = back_sum.reshape(4, 16, 256)
    give = link(part.at[:, pl.ds(pl.multiple_of(8 * other, 8), 8)], part_in, to_chan)
    give.start()

    settle(rims[2])
    for pair in late:
        settle(pair)
    gturn[...] = jnp.transpose(gall[1:17].reshape(256, 256).astype(F32)).astype(BF)
    for cc in range(chans):
        ppad[:, 8 + 8 * cc : 16 + 8 * cc, :] = pbuf[:, cc].astype(F32)
    for j in range(3):
        xfull[:, :, j * 256 : j * 256 + 256] = ppad[:, 7 + j : 23 + j, :].astype(BF)
    rows = pl.multiple_of(32 * quarter, 32)
    chosen = jnp.concatenate([gturn[pl.ds(rows, 32), :], gturn[pl.ds(128 + rows, 32), :]], axis=0)
    for i in range(3):
        for j in range(3):
            cross = jnp.dot(
                chosen, xfull[i : i + 16, :, j * 256 : j * 256 + 256].reshape(256, 256), preferred_element_type=F32
            )
            blocks = (
                cross[32:64, 0:128], cross[0:32, 0:128] + cross[32:64, 128:256], cross[0:32, 128:256]
            )
            for l, block in enumerate(blocks):
                tap = 9 * i + 3 * j + l
                for p in range(2):
                    own_t[p, tap // 14, tap // 7 % 2, tap % 7] = block[16 * p : 16 * p + 16]
    advance("tu")
    field = pre[...]
    sig = 1.0 / (1.0 + jnp.exp(-field))
    pre[...] = 0.125 * (sig * (1.0 + field * (1.0 - sig)))

    give.wait()
    pooled_grad = part[:, pl.ds(pl.multiple_of(8 * c, 8), 8)] + part_in[...]
    wides = []
    for x, fold in enumerate((fold0, fold1)):
        half = pooled_grad[:, :, x * 128 : x * 128 + 128].reshape(32, 128)
        fold[pl.ds(0, 32, 2), :] = half
        fold[pl.ds(1, 32, 2), :] = half
        half = jnp.broadcast_to(fold[...].reshape(4, 1, 16, 128), (4, 2, 16, 128)).reshape(128, 128)
        wides += [half, half]
    grads_mid = (jnp.concatenate(wides, axis=1) * pre[...]).astype(BF)

    def mid_taps(i):
        for j in range(3):
            cross = lax.dot_general(
                xmid[i : i + 8, :, j * 256 : j * 256 + 256].reshape(128, 256), grads_mid,
                (((0,), (0,)), ((), ())), preferred_element_type=F32,
            )
            for l in range(3):
                block = None
                for xo in range(4):
                    xi = xo + l - 1
                    if 0 <= xi < 4:
                        term = cross[xi * 64 : xi * 64 + 64, xo * 128 : xo * 128 + 128]
                        block = term if block is None else block + term
                for n in range(2):
                    unit = 2 * (9 * i + 3 * j + l) + n
                    for p in range(2):
                        acc_m[p, unit // 27, unit % 27] = block[32 * n + 16 * p : 32 * n + 16 * p + 16]

    mid_taps(0)
    mid_taps(1)
    mid_taps(2)
    advance("mntumntumntumntumntumntumnmn")


def fused_device(sizes, volume, kernel_mid, kernel_top, upstream):
    vol = volume[0]
    upper = jnp.transpose(upstream[0, :, :, 0, :], (1, 0, 2)).astype(F32).reshape(16, 128)
    vm = pltpu.VMEM
    block, mid, top = pl.pallas_call(
        functools.partial(fused_body, sizes),
        out_shape=(
            jax.ShapeDtypeStruct((16, 128), F32),
            jax.ShapeDtypeStruct((27, 32, 128), F32),
            jax.ShapeDtypeStruct((27, 4, 32, 128), F32),
        ),
        in_specs=[
            pl.BlockSpec(memory_space=pltpu.VMEM),
            pl.BlockSpec(memory_space=pltpu.HBM),
            pl.BlockSpec(memory_space=pltpu.HBM),
            pl.BlockSpec(memory_space=pltpu.VMEM),
        ],
        out_specs=[pl.BlockSpec(memory_space=pltpu.VMEM)] * 3,
        scratch_shapes=[
            vm((10, 32, 256), F32), vm((18, 2, 8, 256), BF), vm((18, 16, 256), BF), vm((256, 256), BF),
            vm((18, 16, 768), BF), vm((18, 32, 256), F32), vm((6, 32, 256), F32),
            vm((10, 16, 768), BF), vm((6, 16, 768), BF),
            vm((3, 768, 512), BF), vm((3, 256, 768), BF),
            vm((128, 512), F32), vm((64, 128), F32), vm((64, 128), F32),
            vm((4, 16, 256), F32), vm((4, 8, 256), F32),
            vm((27, 64, 128), BF), vm((27, 128, 128), BF), pltpu.SemaphoreType.DMA((2,)),
            vm((2, 2, 2, 7, 16, 128), F32),
            vm((2, 2, 7, 16, 128), BF), vm((2, 2, 7, 16, 128), BF),
            vm((2, 7, 16, 128), BF), vm((2, 7, 16, 128), BF), vm((2, 4, 2, 2, 7, 16, 128), BF),
            vm((2, 2, 28, 16, 128), F32),
            vm((2, 2, 14, 16, 128), BF), vm((2, 2, 14, 16, 128), BF), vm((2, 14, 16, 128), F32),
            vm((2, 14, 16, 128), BF), vm((2, 14, 16, 128), BF),
            vm((2, 7, 16, 128), BF), vm((2, 7, 16, 128), BF), vm((2, 7, 16, 128), BF), vm((2, 7, 16, 128), BF),
            vm((2, 7, 16, 128), BF), vm((2, 7, 16, 128), BF), vm((2, 4, 7, 16, 128), BF),
            pltpu.SemaphoreType.DMA((64,)), pltpu.SemaphoreType.DMA((64,)),
        ],
        compiler_params=pltpu.CompilerParams(
            collective_id=0, has_side_effects=True, vmem_limit_bytes=40 * 1024 * 1024
        ),
        name="fused",
    )(vol, kernel_mid, kernel_top, upper)
    block_out = jnp.transpose(block.reshape(2, 8, 128), (1, 0, 2)).astype(BF)[None, :, :, None, :]
    return (block_out, mid.reshape(864, 128), top.reshape(27, 128, 128))


def solution(mesh):
    sizes = (mesh.shape["sample"], mesh.shape["spatial"], mesh.shape["channel"])

    def per_device(volume, kernel_mid, kernel_top, upstream):
        fits = (
            sizes == (4, 4, 2)
            and volume.shape == (1, 16, 8, 256)
            and kernel_mid.shape == (27, 64, 128)
            and kernel_top.shape == (27, 128, 128)
            and upstream.shape == (1, 8, 2, 1, 128)
        )
        if fits:
            return fused_device(sizes, volume, kernel_mid, kernel_top, upstream)
        return on_device(volume, kernel_mid, kernel_top, upstream)

    return jax.shard_map(
        per_device,
        mesh=mesh,
        in_specs=(
            P("sample", "channel", "spatial", None),
            P(),
            P(None, "channel", None),
            P("sample", None, "spatial", None, "channel"),
        ),
        out_specs=(
            P("sample", None, "spatial", None, "channel"),
            P("channel", None),
            P(None, "channel", None),
        ),
        check_vma=False,
    )
```
